512 devices in a mesh: section: 2 (over core), dp: 256 (over z, y, x).
Axes of the slice: x: 4, y: 8, z: 8, core: 2. Of those that a mesh axis runs over, the one named last changes fastest.
Arguments:
- images: bfloat16 [4, 512, 8, 8, 512], P(None, 'dp'), may hold values from -6 to 6
- cotangent: bfloat16 [4, 512, 8, 8, 512], P(None, 'dp'), may hold values from -0.016479492 to 0.016479492
- counts: int32 [2], P('section'), may hold values from 1 to 4, as said below
- gains: float32 [8, 512], P('section'), may hold values from 0.1 to 1.9
- depthwise: float32 [8, 9, 512], P('section'), may hold values from -2 to 2
- pointwise: bfloat16 [8, 512, 512], P('section'), may hold values from -0.25 to 0.25
Outputs:
- grad_pointwise: float32 [8, 512, 512], P('section')
- grad_depthwise: float32 [8, 9, 512], P('section')
- grad_gains: float32 [8, 512], P('section')
The draws below stay inside these ranges and needn't reach their ends.
Inputs may be any that keep to these rules, and one draw needn't show every extreme that they name: counts[s] is how many cells segment s applies, from its first slot on; at least one segment applies 4 cells.
All inputs are finite; a program needn't handle non-finite values.
Results may differ from the reference program's by a relative error of at most 0.0085.
Values may be sent and summed in bfloat16 or wider, within the bound.
No kernel may reach another device: no remote copies, remote signals or barrier semaphores. Data moves between devices by JAX's collectives and lax.ppermute only.
A program may use at most 64 MiB of HBM per device.

```python
import math
import jax
import jax.numpy as jnp
from jax import lax

C = 512
TAPS = 9
MAXC = 4
MICRO = 4
HEIGHT = 8
WIDTH = 8
BATCH = 512
SECTIONS = 2
SLOTS = 8


def draw_counts(key, part):
    key_counts, key_order = jax.random.split(key)
    drawn_counts = jax.random.randint(key_counts, (SECTIONS,), 1, MAXC + 1)
    shuffled = jax.random.permutation(key_order, SECTIONS)
    drawn_counts = drawn_counts.at[shuffled[0]].set(MAXC)
    return drawn_counts.astype(jnp.int32)


def shard_levels(own_key, shape, cuts, smallest, high):
    level, own = 1.0, jax.random.fold_in(own_key, 6)
    for position, blocks in cuts:
        draws = jnp.exp(jax.random.uniform(jax.random.fold_in(own, position), (blocks,), jnp.float32, smallest / len(cuts), high / len(cuts)))
        level = level * jnp.repeat(draws, shape[position] // blocks).reshape([-1 if axis == position else 1 for axis in range(len(shape))])
    return level


def centred(rng, dims, scale, limit, cuts=(), held_as=jnp.bfloat16):
    level = shard_levels(rng, dims, cuts, -0.22, 0.18) if cuts else 1.0
    values = jax.random.normal(rng, dims, jnp.float32) * scale * level
    return jnp.minimum(jnp.maximum(values, -limit), limit).astype(held_as)


def setup_inputs(seed: int = 0) -> dict:
    seeds = jax.random.split(jax.random.key(seed), 7)
    return {
        "images": centred(seeds[0], (MICRO, BATCH, HEIGHT, WIDTH, C), 1.0, 6.0, ((1, 256),)),
        "cotangent": centred(seeds[1], (MICRO, BATCH, HEIGHT, WIDTH, C), (1.0 / (MICRO * BATCH * HEIGHT * WIDTH) ** 0.5), 0.016479492, ((1, 256),)),
        "counts": draw_counts(jax.random.fold_in(seeds[6], 71), 0),
        "gains": jnp.clip(1.0 + 0.18 * jax.random.normal(seeds[3], (SLOTS, C), jnp.float32), 0.1, 1.9),
        "depthwise": centred(seeds[4], (SLOTS, TAPS, C), TAPS ** -0.5, 2.0, ((0, 2),), jnp.float32),
        "pointwise": centred(seeds[5], (SLOTS, C, C), C ** -0.5, 0.25, ((0, 2),)),
    }


EPSILON = 1e-06

def depth_apply(normed, depth_w):
    kernel = math.isqrt(depth_w.shape[0])
    offset = kernel // 2
    height, map_width = (normed.shape[1], normed.shape[2])
    padded = jnp.pad(normed, ((0, 0), (offset, offset), (offset, offset), (0, 0)))
    summed = jnp.zeros_like(normed)
    for row_tap in range(kernel):
        for col_tap in range(kernel):
            summed = summed + depth_w[row_tap * kernel + col_tap] * padded[:, row_tap:row_tap + height, col_tap:col_tap + map_width]
    return summed

def cell_parts(cell_in, gain_row, depth_w):
    widened = cell_in.astype(jnp.float32)
    inverse = lax.rsqrt(lax.optimization_barrier(jnp.mean(widened * widened, axis=-1, keepdims=True)) + EPSILON)
    normed = widened * inverse * gain_row
    linear = depth_apply(normed, depth_w)
    activated = (linear * jax.nn.sigmoid(linear)).astype(jnp.bfloat16)
    return (widened, inverse, normed, linear, activated)

def cell_forward(cell_in, gain_row, depth_w, point_w):
    widened, inverse, normed, linear, activated = cell_parts(cell_in, gain_row, depth_w)
    channels = point_w.shape[0]
    mixed_sum = jnp.dot(activated.reshape(-1, channels), point_w, preferred_element_type=jnp.float32)
    return (widened + mixed_sum.reshape(widened.shape)).astype(jnp.bfloat16)

def cell_backward(cell_in, grad_out, gain_row, depth_w, point_w):
    widened, inverse, normed, linear, activated = cell_parts(cell_in, gain_row, depth_w)
    channels = point_w.shape[0]
    flat_act = activated.reshape(-1, channels)
    flat_grad = grad_out.reshape(-1, channels)
    grad_point = lax.dot_general(flat_act, flat_grad, (((0,), (0,)), ((), ())), preferred_element_type=jnp.float32)
    grad_act = lax.dot_general(flat_grad, point_w, (((1,), (1,)), ((), ())), preferred_element_type=jnp.float32).reshape(widened.shape)
    sigma = jax.nn.sigmoid(linear)
    grad_linear = grad_act * (sigma * (1.0 + linear * (1.0 - sigma)))
    kernel = math.isqrt(depth_w.shape[0])
    offset = kernel // 2
    height, map_width = (normed.shape[1], normed.shape[2])
    padded = jnp.pad(normed, ((0, 0), (offset, offset), (offset, offset), (0, 0)))
    padded_grad = jnp.pad(grad_linear, ((0, 0), (offset, offset), (offset, offset), (0, 0)))
    tap_list = []
    grad_normed = jnp.zeros_like(grad_linear)
    for row_tap in range(kernel):
        for col_tap in range(kernel):
            tap_list.append(lax.optimization_barrier(jnp.sum(padded[:, row_tap:row_tap + height, col_tap:col_tap + map_width] * grad_linear, axis=(0, 1, 2))))
            row_start = 2 * offset - row_tap
            col_start = 2 * offset - col_tap
            grad_normed = grad_normed + depth_w[row_tap * kernel + col_tap] * padded_grad[:, row_start:row_start + height, col_start:col_start + map_width]
    grad_depth = jnp.stack(tap_list)
    grad_gain = lax.optimization_barrier(jnp.sum(grad_normed * widened * inverse, axis=(0, 1, 2)))
    scaled = grad_normed * gain_row
    grad_in = grad_out.astype(jnp.float32) + inverse * scaled - widened * inverse ** 3 * lax.optimization_barrier(jnp.mean(scaled * widened, axis=-1, keepdims=True))
    return (grad_in.astype(jnp.bfloat16), grad_point, grad_depth, grad_gain)

def reference(images, cotangent, counts, gains, depthwise, pointwise):
    item_shape = images.shape[2:]
    flat_in = images.reshape((-1,) + item_shape)
    flat_cot = cotangent.reshape((-1,) + item_shape)
    total_images = flat_in.shape[0]
    block = math.gcd(total_images, 32)
    blocks_in = flat_in.reshape((total_images // block, block) + item_shape)
    blocks_cot = flat_cot.reshape((total_images // block, block) + item_shape)

    def block_step(totals, pair):
        point_tot, depth_tot, gain_tot = totals
        running, grad_run = pair
        saved = []
        for slot_number in range(SLOTS):
            segment_number = slot_number // MAXC
            cell_number = slot_number % MAXC
            saved.append(running)
            moved = cell_forward(running, gains[slot_number], depthwise[slot_number], pointwise[slot_number])
            running = jnp.where(cell_number < counts[segment_number], moved, running)
        point_list = [None] * SLOTS
        depth_list = [None] * SLOTS
        gain_list = [None] * SLOTS
        for slot_number in reversed(range(SLOTS)):
            segment_number = slot_number // MAXC
            cell_number = slot_number % MAXC
            working = cell_number < counts[segment_number]
            grad_in, grad_point, grad_depth, grad_gain = cell_backward(saved[slot_number], grad_run, gains[slot_number], depthwise[slot_number], pointwise[slot_number])
            grad_run = jnp.where(working, grad_in, grad_run)
            point_list[slot_number] = jnp.where(working, grad_point, jnp.zeros_like(grad_point))
            depth_list[slot_number] = jnp.where(working, grad_depth, jnp.zeros_like(grad_depth))
            gain_list[slot_number] = jnp.where(working, grad_gain, jnp.zeros_like(grad_gain))
        return ((point_tot + jnp.stack(point_list), depth_tot + jnp.stack(depth_list), gain_tot + jnp.stack(gain_list)), None)
    start = (jnp.zeros((SLOTS, C, C), jnp.float32), jnp.zeros((SLOTS, TAPS, C), jnp.float32), jnp.zeros((SLOTS, C), jnp.float32))
    (point_sums, depth_sums, gain_sums), unused_out = lax.scan(block_step, start, (blocks_in, blocks_cot))
    return (point_sums, depth_sums, gain_sums)
```

```python
import jax
import jax.numpy as jnp
from jax import lax
from jax.experimental import pallas as pl
from jax.experimental.pallas import tpu as pltpu
from jax.sharding import Mesh, PartitionSpec as P

EPSILON = 1e-06
f32, bf16 = jnp.float32, jnp.bfloat16
LANES = 128


def cells_kernel(
    counts, where_, images, cotangent, vec_own, vec_far, point_own, point_far,
    kept, sent,
    point, vec, folded, state, normed, inverse, slope, act, grad_run, grad_act, mixed, taps, sems,
):
    half, channels = point_own.shape[0], point_own.shape[2]
    slots = 2 * half
    groups, height, width = images.shape[0], images.shape[2], images.shape[3]
    pixels = height * width
    tiles = channels // LANES
    mine = where_[0] * half
    theirs = half - mine
    copies = [
        pltpu.make_async_copy(point_own, point.at[pl.ds(mine, half)], sems.at[0]),
        pltpu.make_async_copy(point_far, point.at[pl.ds(theirs, half)], sems.at[1]),
    ]
    for copy in copies:
        copy.start()
    vec[pl.ds(mine, half)] = vec_own[...]
    vec[pl.ds(theirs, half)] = vec_far[...]
    for m in range(groups):
        state[m * pixels:(m + 1) * pixels] = images[m, 0].reshape(pixels, channels).astype(f32)
        grad_run[m * pixels:(m + 1) * pixels] = cotangent[m, 0].reshape(pixels, channels).astype(f32)
    for copy in copies:
        copy.wait()

    column = lax.broadcasted_iota(jnp.int32, (width, LANES), 0)
    not_first = column > 0
    not_last = column < width - 1

    def from_left(a):
        return jnp.where(not_first, pltpu.roll(a, 1, 0), 0.0)

    def from_right(a):
        return jnp.where(not_last, pltpu.roll(a, width - 1, 0), 0.0)

    def rows_of(block):
        return [block[h * width:(h + 1) * width] for h in range(height)]

    def active(k):
        return lax.rem(k, half) < counts[lax.div(k, half)]

    def forward(k, carry):
        @pl.when(active(k))
        def _():
            gain = vec[k, 9:10, :]
            for t in range(9):
                folded[k, t:t + 1, :] = vec[k, t:t + 1, :] * gain

            def image(m, c):
                rows = pl.ds(pl.multiple_of(m * pixels, pixels), pixels)
                x = state[rows, :]
                inv = lax.rsqrt(jnp.mean(x * x, axis=-1, keepdims=True) + EPSILON)
                inverse[k, rows, :] = jnp.broadcast_to(inv, (pixels, LANES))
                for j in range(tiles):
                    cs = slice(j * LANES, (j + 1) * LANES)
                    xn = x[:, cs] * inv
                    normed[k, rows, cs] = xn
                    mid = rows_of(xn)
                    left = [from_left(a) for a in mid]
                    right = [from_right(a) for a in mid]
                    w = [jnp.broadcast_to(folded[k, t:t + 1, cs], (width, LANES)) for t in range(9)]
                    acts, slopes = [], []
                    for h in range(height):
                        lin = None
                        for p in range(3):
                            r = h + p - 1
                            if r < 0 or r >= height:
                                continue
                            for q, src in enumerate((left, mid, right)):
                                term = w[p * 3 + q] * src[r]
                                lin = term if lin is None else lin + term
                        sig = 0.5 * jnp.tanh(0.5 * lin) + 0.5
                        a = lin * sig
                        acts.append(a)
                        slopes.append(sig + a * (1.0 - sig))
                    act[k, rows, cs] = jnp.concatenate(acts, axis=0).astype(bf16)
                    slope[k, rows, cs] = jnp.concatenate(slopes, axis=0)
                return c

            lax.fori_loop(0, groups, image, 0)
            mixed[...] = jnp.dot(act[k], point[k], preferred_element_type=f32)
            state[...] = (state[...] + mixed[...]).astype(bf16).astype(f32)
        return carry

    lax.fori_loop(0, slots, forward, 0)

    def backward(i, carry):
        k = slots - 1 - i

        home = lax.div(k, half) == where_[0]
        cell = lax.rem(k, half)

        def store(rows, value):
            @pl.when(home)
            def _():
                kept[cell, rows, :] = value

            @pl.when(jnp.logical_not(home))
            def _():
                sent[cell, rows, :] = value

        @pl.when(jnp.logical_not(active(k)))
        def _():
            store(slice(0, channels + 16), jnp.zeros((channels + 16, channels), bf16))

        @pl.when(active(k))
        def _():
            g = grad_run[...].astype(bf16)
            grad_act[...] = lax.dot_general(g, point[k], (((1,), (1,)), ((), ())), preferred_element_type=f32)
            store(
                slice(0, channels),
                lax.dot_general(act[k], g, (((0,), (0,)), ((), ())), preferred_element_type=f32).astype(bf16),
            )
            taps[...] = jnp.zeros_like(taps)

            def image(m, c):
                rows = pl.ds(pl.multiple_of(m * pixels, pixels), pixels)
                total = jnp.zeros((pixels, LANES), f32)
                for j in range(tiles):
                    cs = slice(j * LANES, (j + 1) * LANES)
                    gl = grad_act[rows, cs] * slope[k, rows, cs]
                    xn = normed[k, rows, cs]
                    mid = rows_of(gl)
                    src = ([from_right(a) for a in mid], mid, [from_left(a) for a in mid])
                    xr = rows_of(xn)
                    w = [jnp.broadcast_to(folded[k, t:t + 1, cs], (width, LANES)) for t in range(9)]
                    us = []
                    for h in range(height):
                        u = None
                        for p in range(3):
                            r = h - p + 1
                            if r < 0 or r >= height:
                                continue
                            for q in range(3):
                                term = w[p * 3 + q] * src[q][r]
                                u = term if u is None else u + term
                        us.append(u)
                    for p in range(3):
                        for q in range(3):
                            t = p * 3 + q
                            s = None
                            for h in range(height):
                                r = h - p + 1
                                if r < 0 or r >= height:
                                    continue
                                term = xr[h] * src[q][r]
                                s = term if s is None else s + term
                            taps[t * 8:(t + 1) * 8, cs] += s
                    u = jnp.concatenate(us, axis=0)
                    mixed[rows, cs] = u
                    total = total + u * xn
                mean = jnp.sum(total, axis=-1, keepdims=True) * (1.0 / channels)
                inv = inverse[k, rows, :]
                mean_b = jnp.broadcast_to(mean, (pixels, LANES))
                for j in range(tiles):
                    cs = slice(j * LANES, (j + 1) * LANES)
                    gx = grad_run[rows, cs] + inv * (mixed[rows, cs] - normed[k, rows, cs] * mean_b)
                    grad_run[rows, cs] = gx.astype(bf16).astype(f32)
                return c

            lax.fori_loop(0, groups, image, 0)
            gain = vec[k, 9:10, :]
            grad_gain = jnp.zeros((1, channels), f32)
            parts = []
            for t in range(9):
                summed = jnp.sum(taps[t * 8:(t + 1) * 8, :], axis=0, keepdims=True)
                parts.append(summed * gain)
                grad_gain = grad_gain + vec[k, t:t + 1, :] * summed
            parts += [grad_gain, jnp.zeros((6, channels), f32)]
            store(slice(channels, channels + 16), jnp.concatenate(parts, axis=0).astype(bf16))
        return carry

    lax.fori_loop(0, slots, backward, 0)


def run_cells(counts, section, images, cotangent, vec_own, vec_far, point_own, point_far):
    slots = 2 * point_own.shape[0]
    groups, unused, height, width, channels = images.shape
    total = groups * height * width
    share = (groups, 1, height, width, channels)
    vec_shape = (slots, 10, channels)
    packed = (slots // 2, channels + 16, channels)
    spec = pltpu.PrefetchScalarGridSpec(
        num_scalar_prefetch=2,
        grid=(1,),
        in_specs=[
            pl.BlockSpec(share, lambda i, c, s: (0, s[0], 0, 0, 0)),
            pl.BlockSpec(share, lambda i, c, s: (0, s[0], 0, 0, 0)),
            pl.BlockSpec(vec_own.shape, lambda i, c, s: (0, 0, 0)),
            pl.BlockSpec(vec_far.shape, lambda i, c, s: (0, 0, 0)),
            pl.BlockSpec(memory_space=pl.ANY),
            pl.BlockSpec(memory_space=pl.ANY),
        ],
        out_specs=[
            pl.BlockSpec(packed, lambda i, c, s: (0, 0, 0)),
            pl.BlockSpec(packed, lambda i, c, s: (0, 0, 0)),
        ],
        scratch_shapes=[
            pltpu.VMEM((slots, channels, channels), bf16),
            pltpu.VMEM(vec_shape, f32),
            pltpu.VMEM((slots, 9, channels), f32),
            pltpu.VMEM((total, channels), f32),
            pltpu.VMEM((slots, total, channels), f32),
            pltpu.VMEM((slots, total, LANES), f32),
            pltpu.VMEM((slots, total, channels), f32),
            pltpu.VMEM((slots, total, channels), bf16),
            pltpu.VMEM((total, channels), f32),
            pltpu.VMEM((total, channels), f32),
            pltpu.VMEM((total, channels), f32),
            pltpu.VMEM((72, channels), f32),
            pltpu.SemaphoreType.DMA((2,)),
        ],
    )
    return pl.pallas_call(
        cells_kernel,
        grid_spec=spec,
        out_shape=[
            jax.ShapeDtypeStruct(packed, bf16),
            jax.ShapeDtypeStruct(packed, bf16),
        ],
        compiler_params=pltpu.CompilerParams(vmem_limit_bytes=56 << 20),
        name="cells",
    )(counts, section, images, cotangent, vec_own, vec_far, point_own, point_far)


def swapped(block):
    return lax.ppermute(block, "section", [(0, 1), (1, 0)])


def local(images, cotangent, counts, gains, depthwise, pointwise):
    cells, channels = gains.shape
    section = lax.axis_index("section").astype(jnp.int32)
    vec_own = jnp.concatenate([depthwise, gains[:, None, :]], axis=1)
    counts_far = swapped(counts)
    both = jnp.where(section == 0, jnp.concatenate([counts, counts_far]), jnp.concatenate([counts_far, counts]))
    kept, sent = run_cells(
        both, section[None], images, cotangent, vec_own, swapped(vec_own), pointwise, swapped(pointwise)
    )
    summed = (kept.astype(f32) + swapped(sent).astype(f32)).astype(bf16)

    along = lax.axis_size("x")
    plane = lax.axis_size("z") * lax.axis_size("y")
    parts = lax.all_to_all(summed, "x", 0, 0, tiled=True)
    cell = jnp.sum(parts.astype(f32).reshape((along,) + summed.shape[1:]), axis=0)
    point, vec = cell[:channels], cell[channels:channels + 16]
    strip = jnp.pad(vec.reshape(-1, LANES), ((0, channels - vec.size // LANES), (0, 0)))
    wide = jnp.concatenate([point, strip], axis=1).astype(bf16).reshape(plane, channels // plane, channels + LANES)
    piece = jnp.sum(lax.all_to_all(wide, ("z", "y"), 0, 0, tiled=True).astype(f32), axis=0).astype(bf16)

    whole = lax.all_to_all(jnp.broadcast_to(piece, wide.shape), ("z", "y"), 0, 0, tiled=True)
    whole = whole.reshape(1, channels, channels + LANES)
    whole = lax.all_to_all(jnp.broadcast_to(whole, (along,) + whole.shape[1:]), "x", 0, 0, tiled=True)
    out = whole.astype(f32)
    small = out[:, :16 * channels // LANES, channels:].reshape(cells, 16, channels)
    return out[:, :, :channels], small[:, :9], small[:, 9]


def solution(mesh):
    grid = Mesh(mesh.devices.reshape(2, 8, 8, 4), ("section", "z", "y", "x"))
    data = ("z", "y", "x")
    placed = (
        P(None, data, None, None, None),
        P(None, data, None, None, None),
        P("section"),
        P("section", None),
        P("section", None, None),
        P("section", None, None),
    )
    return jax.shard_map(
        local,
        mesh=grid,
        in_specs=placed,
        out_specs=(P("section", None, None), P("section", None, None), P("section", None)),
        check_vma=False,
    )
```

```python
import jax
import jax.numpy as jnp
from jax import lax
from jax.experimental import pallas as pl
from jax.experimental.pallas import tpu as pltpu
from jax.sharding import Mesh, PartitionSpec as P

EPSILON = 1e-06
f32, bf16 = jnp.float32, jnp.bfloat16
LANES = 128
QUARTERS = 4
NEAR = ("zl", "yl", "x")
FAR = ("zh", "yh")


def cells_kernel(
    where_, images, cotangent, vec_own, vec_far, point_own, point_far,
    kept, sent,
    point, vec, folded, state, normed, inverse, slope, act, grad_run, grad_act, mixed, taps, sems,
):
    half, channels = point_own.shape[0], point_own.shape[2]
    quarters = kept.shape[0] // half
    block = channels // quarters
    slots = 2 * half
    groups, height, width = images.shape[0], images.shape[2], images.shape[3]
    pixels = height * width
    tiles = channels // LANES
    mine = where_[0] * half
    theirs = half - mine
    copies = [
        pltpu.make_async_copy(point_own, point.at[pl.ds(mine, half)], sems.at[0]),
        pltpu.make_async_copy(point_far, point.at[pl.ds(theirs, half)], sems.at[1]),
    ]
    for copy in copies:
        copy.start()
    vec[pl.ds(mine, half)] = vec_own[...]
    vec[pl.ds(theirs, half)] = vec_far[...]
    for m in range(groups):
        state[m * pixels:(m + 1) * pixels] = images[m, 0].reshape(pixels, channels).astype(f32)
        grad_run[m * pixels:(m + 1) * pixels] = cotangent[m, 0].reshape(pixels, channels).astype(f32)
    column = lax.broadcasted_iota(jnp.int32, (width, LANES), 0)
    not_first = column > 0
    not_last = column < width - 1

    def from_left(a):
        return jnp.where(not_first, pltpu.roll(a, 1, 0), 0.0)

    def from_right(a):
        return jnp.where(not_last, pltpu.roll(a, width - 1, 0), 0.0)

    def rows_of(block):
        return [block[h * width:(h + 1) * width] for h in range(height)]

    count_own = jnp.max(vec_own[0, 10:11, :])
    count_far = jnp.max(vec_far[0, 10:11, :])

    def active(k):
        limit = jnp.where(lax.div(k, half) == where_[0], count_own, count_far)
        return lax.rem(k, half).astype(f32) < limit

    def forward(k, carry):
        @pl.when(active(k))
        def _():
            gain = vec[k, 9:10, :]
            for t in range(9):
                folded[k, t:t + 1, :] = vec[k, t:t + 1, :] * gain

            def image(m, c):
                rows = pl.ds(pl.multiple_of(m * pixels, pixels), pixels)
                x = state[rows, :]
                inv = lax.rsqrt(jnp.mean(x * x, axis=-1, keepdims=True) + EPSILON)
                inverse[k, rows, :] = jnp.broadcast_to(inv, (pixels, LANES))
                for j in range(tiles):
                    cs = slice(j * LANES, (j + 1) * LANES)
                    xn = x[:, cs] * inv
                    normed[k, rows, cs] = xn
                    mid = rows_of(xn)
                    left = [from_left(a) for a in mid]
                    right = [from_right(a) for a in mid]
                    w = [jnp.broadcast_to(folded[k, t:t + 1, cs], (width, LANES)) for t in range(9)]
                    acts, slopes = [], []
                    for h in range(height):
                        lin = None
                        for p in range(3):
                            r = h + p - 1
                            if r < 0 or r >= height:
                                continue
                            for q, src in enumerate((left, mid, right)):
                                term = w[p * 3 + q] * src[r]
                                lin = term if lin is None else lin + term
                        sig = 0.5 * jnp.tanh(0.5 * lin) + 0.5
                        a = lin * sig
                        acts.append(a)
                        slopes.append(sig + a * (1.0 - sig))
                    act[k, rows, cs] = jnp.concatenate(acts, axis=0).astype(bf16)
                    slope[k, rows, cs] = jnp.concatenate(slopes, axis=0)
                return c

            lax.fori_loop(0, groups, image, 0)

        @pl.when(k == 0)
        def _():
            for copy in copies:
                copy.wait()

        @pl.when(active(k))
        def _():
            mixed[...] = jnp.dot(act[k], point[k], preferred_element_type=f32)
            state[...] = (state[...] + mixed[...]).astype(bf16).astype(f32)
        return carry

    lax.fori_loop(0, slots, forward, 0)

    def backward(i, carry):
        k = slots - 1 - i

        home = lax.div(k, half) == where_[0]
        cell = lax.rem(k, half)

        def store(first, count, value):
            rows = slice(first, first + count)

            @pl.when(home)
            def _():
                for r in range(quarters):
                    kept[quarters * cell + r, rows, :] = value[r * count:(r + 1) * count]

            @pl.when(jnp.logical_not(home))
            def _():
                for r in range(quarters):
                    sent[quarters * cell + r, rows, :] = value[r * count:(r + 1) * count]

        @pl.when(jnp.logical_not(active(k)))
        def _():
            store(0, block, jnp.zeros((channels, channels), bf16))
            store(block, 8, jnp.zeros((quarters * 8, channels), bf16))

        @pl.when(active(k))
        def _():
            g = grad_run[...].astype(bf16)
            grad_act[...] = lax.dot_general(g, point[k], (((1,), (1,)), ((), ())), preferred_element_type=f32)
            store(
                0,
                block,
                lax.dot_general(act[k], g, (((0,), (0,)), ((), ())), preferred_element_type=f32).astype(bf16),
            )
            taps[...] = jnp.zeros_like(taps)

            def image(m, c):
                rows = pl.ds(pl.multiple_of(m * pixels, pixels), pixels)
                total = jnp.zeros((pixels, LANES), f32)
                for j in range(tiles):
                    cs = slice(j * LANES, (j + 1) * LANES)
                    gl = grad_act[rows, cs] * slope[k, rows, cs]
                    xn = normed[k, rows, cs]
                    mid = rows_of(gl)
                    src = ([from_right(a) for a in mid], mid, [from_left(a) for a in mid])
                    xr = rows_of(xn)
                    w = [jnp.broadcast_to(folded[k, t:t + 1, cs], (width, LANES)) for t in range(9)]
                    us = []
                    for h in range(height):
                        u = None
                        for p in range(3):
                            r = h - p + 1
                            if r < 0 or r >= height:
                                continue
                            for q in range(3):
                                term = w[p * 3 + q] * src[q][r]
                                u = term if u is None else u + term
                        us.append(u)
                    for p in range(3):
                        for q in range(3):
                            t = p * 3 + q
                            s = None
                            for h in range(height):
                                r = h - p + 1
                                if r < 0 or r >= height:
                                    continue
                                term = xr[h] * src[q][r]
                                s = term if s is None else s + term
                            taps[t * 8:(t + 1) * 8, cs] += s
                    u = jnp.concatenate(us, axis=0)
                    mixed[rows, cs] = u
                    total = total + u * xn
                mean = jnp.sum(total, axis=-1, keepdims=True) * (1.0 / channels)
                inv = inverse[k, rows, :]
                mean_b = jnp.broadcast_to(mean, (pixels, LANES))
                for j in range(tiles):
                    cs = slice(j * LANES, (j + 1) * LANES)
                    gx = grad_run[rows, cs] + inv * (mixed[rows, cs] - normed[k, rows, cs] * mean_b)
                    grad_run[rows, cs] = gx.astype(bf16).astype(f32)
                return c

            lax.fori_loop(0, groups, image, 0)
            gain = vec[k, 9:10, :]
            grad_gain = jnp.zeros((1, channels), f32)
            parts = []
            for t in range(9):
                summed = jnp.sum(taps[t * 8:(t + 1) * 8, :], axis=0, keepdims=True)
                parts.append(summed * gain)
                grad_gain = grad_gain + vec[k, t:t + 1, :] * summed
            parts += [grad_gain, jnp.zeros((2, channels), f32)]
            spread = []
            for r in range(quarters):
                spread += parts[r * 3:r * 3 + 3] + [jnp.zeros((5, channels), f32)]
            store(block, 8, jnp.concatenate(spread[:15] + [jnp.zeros((7, channels), f32)], axis=0).astype(bf16))
        return carry

    lax.fori_loop(0, slots, backward, 0)


def run_cells(section, images, cotangent, vec_own, vec_far, point_own, point_far):
    slots = 2 * point_own.shape[0]
    groups, unused, height, width, channels = images.shape
    total = groups * height * width
    share = (groups, 1, height, width, channels)
    vec_shape = (slots, 11, channels)
    packed = (QUARTERS * slots // 2, channels // QUARTERS + 8, channels)
    spec = pltpu.PrefetchScalarGridSpec(
        num_scalar_prefetch=1,
        grid=(1,),
        in_specs=[
            pl.BlockSpec(share, lambda i, s: (0, s[0], 0, 0, 0)),
            pl.BlockSpec(share, lambda i, s: (0, s[0], 0, 0, 0)),
            pl.BlockSpec(vec_own.shape, lambda i, s: (0, 0, 0)),
            pl.BlockSpec(vec_far.shape, lambda i, s: (0, 0, 0)),
            pl.BlockSpec(memory_space=pl.ANY),
            pl.BlockSpec(memory_space=pl.ANY),
        ],
        out_specs=[
            pl.BlockSpec(packed, lambda i, s: (0, 0, 0)),
            pl.BlockSpec(packed, lambda i, s: (0, 0, 0)),
        ],
        scratch_shapes=[
            pltpu.VMEM((slots, channels, channels), bf16),
            pltpu.VMEM(vec_shape, f32),
            pltpu.VMEM((slots, 9, channels), f32),
            pltpu.VMEM((total, channels), f32),
            pltpu.VMEM((slots, total, channels), f32),
            pltpu.VMEM((slots, total, LANES), f32),
            pltpu.VMEM((slots, total, channels), f32),
            pltpu.VMEM((slots, total, channels), bf16),
            pltpu.VMEM((total, channels), f32),
            pltpu.VMEM((total, channels), f32),
            pltpu.VMEM((total, channels), f32),
            pltpu.VMEM((72, channels), f32),
            pltpu.SemaphoreType.DMA((2,)),
        ],
    )
    return pl.pallas_call(
        cells_kernel,
        grid_spec=spec,
        out_shape=[
            jax.ShapeDtypeStruct(packed, bf16),
            jax.ShapeDtypeStruct(packed, bf16),
        ],
        compiler_params=pltpu.CompilerParams(vmem_limit_bytes=56 << 20),
        name="cells",
    )(section, images, cotangent, vec_own, vec_far, point_own, point_far)


def swapped(block):
    return lax.ppermute(block, "section", [(0, 1), (1, 0)])


def exchanged(block, axes):
    return lax.all_to_all(block, axes, 0, 0, tiled=True)


def added(blocks):
    return jnp.sum(blocks.astype(f32), axis=0)


def local(images, cotangent, counts, gains, depthwise, pointwise):
    cells, channels = gains.shape
    section = lax.axis_index("section").astype(jnp.int32)
    point_far = swapped(pointwise)
    vec_own = jnp.concatenate(
        [depthwise, gains[:, None, :], jnp.broadcast_to(counts.astype(f32)[:, None, None], (cells, 1, channels))],
        axis=1,
    )
    vec_far = swapped(vec_own)
    kept, sent = run_cells(section[None], images, cotangent, vec_own, vec_far, pointwise, point_far)
    summed = (kept.astype(f32) + swapped(sent).astype(f32)).astype(bf16)

    near, rows, unused = summed.shape
    rows -= 8
    far = lax.axis_size(FAR)
    part = added(exchanged(summed, NEAR))
    strip = part[rows:rows + 4].reshape(-1, LANES)
    strip = jnp.pad(strip, ((0, rows - strip.shape[0]), (0, 0)))
    wide = jnp.concatenate([part[:rows], strip], axis=1).astype(bf16).reshape(far, rows // far, channels + LANES)
    piece = added(exchanged(wide, FAR)).astype(bf16)

    back = exchanged(jnp.broadcast_to(piece, wide.shape), FAR).reshape(rows, channels + LANES)
    small = back[:32, channels:].reshape(8, channels)
    back = jnp.concatenate([back[:, :channels], small], axis=0)
    out = exchanged(jnp.broadcast_to(back, summed.shape), NEAR).astype(f32)
    small = out[:, rows:rows + 3].reshape(cells, 3 * QUARTERS, channels)
    return out[:, :rows].reshape(cells, channels, channels), small[:, :9], small[:, 9]


def solution(mesh):
    grid = Mesh(mesh.devices.reshape(2, 4, 2, 4, 2, 4), ("section", "zh", "zl", "yh", "yl", "x"))
    data = ("zh", "zl", "yh", "yl", "x")
    placed = (
        P(None, data, None, None, None),
        P(None, data, None, None, None),
        P("section"),
        P("section", None),
        P("section", None, None),
        P("section", None, None),
    )
    return jax.shard_map(
        local,
        mesh=grid,
        in_specs=placed,
        out_specs=(P("section", None, None), P("section", None, None), P("section", None)),
        check_vma=False,
    )
```

```python
from functools import partial

import jax
import jax.numpy as jnp
from jax import lax
from jax.experimental import pallas as pl
from jax.experimental.pallas import tpu as pltpu
from jax.sharding import Mesh, PartitionSpec as P

EPSILON = 1e-06
f32, bf16 = jnp.float32, jnp.bfloat16
LANES = 128
QUARTERS = 4
NEAR = ("zl", "yl", "x")
FAR = ("zh", "yh")


def cells_kernel(
    where_, images, cotangent, vec_own, vec_far, point_own, point_far,
    kept, sent,
    point, vec, folded, packed, grads, final,
    state_a, state_b, normed_a, normed_b, inverse_a, inverse_b, slope_a, slope_b, act_a, act_b,
    grad_act_a, grad_act_b, back_a, back_b, taps_a, taps_b, sems, out_sems,
):
    half, channels = point_own.shape[0], point_own.shape[2]
    slots = 2 * half
    block = channels // QUARTERS
    groups, height, width = images.shape[0], images.shape[2], images.shape[3]
    pixels = height * width
    share = groups // 2
    span = share * pixels
    tiles = channels // LANES
    state, normed, inverse = (state_a, state_b), (normed_a, normed_b), (inverse_a, inverse_b)
    slope, act, grad_act = (slope_a, slope_b), (act_a, act_b), (grad_act_a, grad_act_b)
    back, taps = (back_a, back_b), (taps_a, taps_b)

    mine = where_[0] * half
    theirs = half - mine
    def fetch(k):
        @pl.when(k // half == where_[0])
        def _():
            pltpu.make_async_copy(point_own.at[k % half], point.at[k], sems.at[k]).start()

        @pl.when(k // half != where_[0])
        def _():
            pltpu.make_async_copy(point_far.at[k % half], point.at[k], sems.at[k]).start()

    def arrived(k):
        pltpu.make_async_copy(point_own.at[0], point.at[k], sems.at[k]).wait()

    fetch(0)
    last = pltpu.make_async_copy(cotangent.at[:, where_[0]], final, sems.at[slots])
    for k in range(1, slots):
        fetch(k)
    last.start()
    vec[pl.ds(mine, half)] = vec_own[...]
    vec[pl.ds(theirs, half)] = vec_far[...]
    count_own = jnp.max(vec_own[0, 10:11, :]).astype(jnp.int32)
    count_far = jnp.max(vec_far[0, 10:11, :]).astype(jnp.int32)
    first = jnp.where(where_[0] == 0, count_own, count_far)
    total = count_own + count_far

    def slot_of(i):
        return jnp.where(i < first, i, half + i - first)

    for k in range(slots):
        for t in range(9):
            folded[k, t:t + 1, :] = vec[k, t:t + 1, :] * vec[k, 9:10, :]
    for m in range(groups):
        rows = slice(m % share * pixels, (m % share + 1) * pixels)
        state[m // share][rows] = images[m, 0].reshape(pixels, channels).astype(f32)

    column = lax.broadcasted_iota(jnp.int32, (width, LANES), 0)
    not_first = column > 0
    not_last = column < width - 1

    def from_left(a):
        return jnp.where(not_first, pltpu.roll(a, 1, 0), 0.0)

    def from_right(a):
        return jnp.where(not_last, pltpu.roll(a, width - 1, 0), 0.0)

    def rows_of(values):
        return [values[h * width:(h + 1) * width] for h in range(height)]

    def taps_of(k, cs):
        return [jnp.broadcast_to(folded[k, t:t + 1, cs], (width, LANES)) for t in range(9)]

    def convolve(k, s):
        for m in range(share):
            rows = slice(m * pixels, (m + 1) * pixels)
            x = state[s][rows, :]
            inv = lax.rsqrt(jnp.mean(x * x, axis=-1, keepdims=True) + EPSILON)
            inv = jnp.broadcast_to(inv, (pixels, LANES))
            inverse[s][k, rows, :] = inv
            for j in range(tiles):
                cs = slice(j * LANES, (j + 1) * LANES)
                xn = x[:, cs] * inv
                normed[s][k, rows, cs] = xn
                mid = rows_of(xn)
                src = ([from_left(a) for a in mid], mid, [from_right(a) for a in mid])
                w = taps_of(k, cs)
                acts, slopes = [], []
                for h in range(height):
                    lin = None
                    for p in range(3):
                        r = h + p - 1
                        if r < 0 or r >= height:
                            continue
                        for q in range(3):
                            term = w[p * 3 + q] * src[q][r]
                            lin = term if lin is None else lin + term
                    sig = 0.5 * jnp.tanh(0.5 * lin) + 0.5
                    a = lin * sig
                    acts.append(a)
                    slopes.append(sig + a * (1.0 - sig))
                act[s][k, rows, cs] = jnp.concatenate(acts, axis=0).astype(bf16)
                slope[s][k, rows, cs] = jnp.concatenate(slopes, axis=0)

    def project(k, s):
        for n in range(0, channels, 256):
            cs = slice(n, n + 256)
            mixed = jnp.dot(act[s][k], point[k, :, cs], preferred_element_type=f32)
            state[s][:, cs] = (state[s][:, cs] + mixed).astype(bf16).astype(f32)

    convolve(0, 0)

    def forward(i, carry):
        k = slot_of(i)
        arrived(k)
        project(k, 0)
        convolve(k, 1)
        project(k, 1)
        convolve(slot_of(i + 1), 0)
        return carry

    lax.fori_loop(0, total - 1, forward, 0)
    convolve(slot_of(total - 1), 1)
    arrived(slot_of(total - 1))
    last.wait()

    def pull_back(k, s, side):
        for n in range(0, channels, 256):
            cs = slice(n, n + 256)
            grad_act[s][:, cs] = lax.dot_general(
                grads[side, s * span:(s + 1) * span, :], point[k, cs, :],
                (((1,), (1,)), ((), ())), preferred_element_type=f32,
            )

    def unconvolve(k, s, side):
        totals = [None] * share
        for j in range(tiles):
            cs = slice(j * LANES, (j + 1) * LANES)
            w = taps_of(k, cs)
            sums = [None] * 9
            for m in range(share):
                rows = slice(m * pixels, (m + 1) * pixels)
                gl = grad_act[s][rows, cs] * slope[s][k, rows, cs]
                xn = normed[s][k, rows, cs]
                xr = rows_of(xn)
                mid = rows_of(gl)
                src = ([from_right(a) for a in mid], mid, [from_left(a) for a in mid])
                us = []
                for h in range(height):
                    u = None
                    for p in range(3):
                        r = h - p + 1
                        if r < 0 or r >= height:
                            continue
                        for q in range(3):
                            t = p * 3 + q
                            term = w[t] * src[q][r]
                            u = term if u is None else u + term
                            term = xr[h] * src[q][r]
                            sums[t] = term if sums[t] is None else sums[t] + term
                    us.append(u)
                u = jnp.concatenate(us, axis=0)
                back[s][rows, cs] = u
                totals[m] = u * xn if totals[m] is None else totals[m] + u * xn
            for t in range(9):
                taps[s][t * 8:(t + 1) * 8, cs] = sums[t]
        for m in range(share):
            rows = slice(m * pixels, (m + 1) * pixels)
            there = slice(s * span + m * pixels, s * span + (m + 1) * pixels)
            mean = jnp.sum(totals[m], axis=-1, keepdims=True) * (1.0 / channels)
            mean = jnp.broadcast_to(mean, (pixels, LANES))
            inv = inverse[s][k, rows, :]
            for j in range(tiles):
                cs = slice(j * LANES, (j + 1) * LANES)
                gx = inv * (back[s][rows, cs] - normed[s][k, rows, cs] * mean)
                gx = grads[side, there, cs].astype(f32) + gx
                grads[1 - side, there, cs] = gx.astype(bf16)

    def weigh(k, side):
        both = jnp.concatenate([act[0][k], act[1][k]], axis=0)
        g = grads[side]
        for r in range(QUARTERS):
            packed[QUARTERS * k + r, :block, :] = lax.dot_general(
                both[:, r * block:(r + 1) * block], g, (((0,), (0,)), ((), ())), preferred_element_type=f32
            ).astype(bf16)

    def summarise(k):
        gain = vec[k, 9:10, :]
        grad_gain = jnp.zeros((1, channels), f32)
        parts = []
        for t in range(9):
            both = taps[0][t * 8:(t + 1) * 8, :] + taps[1][t * 8:(t + 1) * 8, :]
            summed = jnp.sum(both, axis=0, keepdims=True)
            parts.append(summed * gain)
            grad_gain = grad_gain + vec[k, t:t + 1, :] * summed
        parts.append(grad_gain)
        for r in range(QUARTERS):
            some = parts[r * 3:r * 3 + 3]
            some = some + [jnp.zeros((8 - len(some), channels), f32)]
            packed[QUARTERS * k + r, block:block + 8, :] = jnp.concatenate(some, axis=0).astype(bf16)

    def send_out(k):
        cell = lax.rem(k, half)
        inside = packed.at[pl.ds(QUARTERS * k, QUARTERS)]
        outside = pl.ds(QUARTERS * cell, QUARTERS)

        @pl.when(lax.div(k, half) == where_[0])
        def _():
            pltpu.make_async_copy(inside, kept.at[outside], out_sems.at[k]).start()

        @pl.when(lax.div(k, half) != where_[0])
        def _():
            pltpu.make_async_copy(inside, sent.at[outside], out_sems.at[k]).start()

    for m in range(groups):
        grads[0, m * pixels:(m + 1) * pixels, :] = final[m].reshape(pixels, channels)
    pull_back(slot_of(total - 1), 0, 0)

    def backward(n, carry):
        i = total - 1 - n
        k = slot_of(i)
        side = lax.rem(n, 2)
        pull_back(k, 1, side)
        unconvolve(k, 0, side)
        weigh(k, side)
        pull_back(slot_of(jnp.maximum(i - 1, 0)), 0, 1 - side)
        unconvolve(k, 1, side)
        summarise(k)
        send_out(k)
        return carry

    lax.fori_loop(0, total, backward, 0)

    def idle(k, carry):
        @pl.when(lax.rem(k, half) >= jnp.where(k < half, first, total - first))
        def _():
            arrived(k)
            packed[pl.ds(QUARTERS * k, QUARTERS)] = jnp.zeros((QUARTERS, block + 8, channels), bf16)
            send_out(k)
        return carry

    lax.fori_loop(0, slots, idle, 0)
    for k in range(slots):
        pltpu.make_async_copy(
            packed.at[QUARTERS * k:QUARTERS * (k + 1)], kept.at[0:QUARTERS], out_sems.at[k]
        ).wait()


def run_cells(section, images, cotangent, vec_own, vec_far, point_own, point_far):
    half = point_own.shape[0]
    slots = 2 * half
    groups, unused, height, width, channels = images.shape
    total = groups * height * width
    span = total // 2
    share = (groups, 1, height, width, channels)
    out = jax.ShapeDtypeStruct((QUARTERS * half, channels // QUARTERS + 8, channels), bf16)

    def pair(shape, dtype):
        return [pltpu.VMEM(shape, dtype)] * 2

    spec = pltpu.PrefetchScalarGridSpec(
        num_scalar_prefetch=1,
        grid=(1,),
        in_specs=[
            pl.BlockSpec(share, lambda i, s: (0, s[0], 0, 0, 0)),
            pl.BlockSpec(memory_space=pl.ANY),
            pl.BlockSpec(vec_own.shape, lambda i, s: (0, 0, 0)),
            pl.BlockSpec(vec_far.shape, lambda i, s: (0, 0, 0)),
            pl.BlockSpec(memory_space=pl.ANY),
            pl.BlockSpec(memory_space=pl.ANY),
        ],
        out_specs=[pl.BlockSpec(memory_space=pl.ANY)] * 2,
        scratch_shapes=[
            pltpu.VMEM((slots, channels, channels), bf16),
            pltpu.VMEM((slots, 11, channels), f32),
            pltpu.VMEM((slots, 9, channels), f32),
            pltpu.VMEM((QUARTERS * slots, channels // QUARTERS + 8, channels), bf16),
            pltpu.VMEM((2, total, channels), bf16),
            pltpu.VMEM((groups, height, width, channels), bf16),
            *pair((span, channels), f32),
            *pair((slots, span, channels), f32),
            *pair((slots, span, LANES), f32),
            *pair((slots, span, channels), f32),
            *pair((slots, span, channels), bf16),
            *pair((span, channels), f32),
            *pair((span, channels), f32),
            *pair((72, channels), f32),
            pltpu.SemaphoreType.DMA((slots + 1,)),
            pltpu.SemaphoreType.DMA((slots,)),
        ],
    )
    return pl.pallas_call(
        cells_kernel,
        grid_spec=spec,
        out_shape=[out, out],
        compiler_params=pltpu.CompilerParams(vmem_limit_bytes=56 << 20),
        name="cells",
    )(section, images, cotangent, vec_own, vec_far, point_own, point_far)


def swapped(block):
    return lax.ppermute(block, "section", [(0, 1), (1, 0)])


def exchanged(block, axes):
    return lax.all_to_all(block, axes, 0, 0, tiled=True)


def added(blocks):
    return jnp.sum(blocks.astype(f32), axis=0)


def local(images, cotangent, counts, gains, depthwise, pointwise):
    cells, channels = gains.shape
    section = lax.axis_index("section").astype(jnp.int32)
    point_far = swapped(pointwise)
    vec_own = jnp.concatenate(
        [depthwise, gains[:, None, :], jnp.broadcast_to(counts.astype(f32)[:, None, None], (cells, 1, channels))],
        axis=1,
    )
    vec_far = swapped(vec_own)
    kept, sent = run_cells(section[None], images, cotangent, vec_own, vec_far, pointwise, point_far)
    summed = (kept.astype(f32) + swapped(sent).astype(f32)).astype(bf16)

    near, rows, unused = summed.shape
    rows -= 8
    far = lax.axis_size(FAR)
    part = added(exchanged(summed, NEAR))
    strip = part[rows:rows + 4].reshape(-1, LANES)
    strip = jnp.pad(strip, ((0, rows - strip.shape[0]), (0, 0)))
    wide = jnp.concatenate([part[:rows], strip], axis=1).astype(bf16).reshape(far, rows // far, channels + LANES)
    piece = added(exchanged(wide, FAR)).astype(bf16)

    back = exchanged(jnp.broadcast_to(piece, wide.shape), FAR).reshape(rows, channels + LANES)
    small = back[:32, channels:].reshape(8, channels)
    back = jnp.concatenate([back[:, :channels], small], axis=0)
    out = exchanged(jnp.broadcast_to(back, summed.shape), NEAR).astype(f32)
    small = out[:, rows:rows + 3].reshape(cells, 3 * QUARTERS, channels)
    return out[:, :rows].reshape(cells, channels, channels), small[:, :9], small[:, 9]


def solution(mesh):
    grid = Mesh(mesh.devices.reshape(2, 4, 2, 4, 2, 4), ("section", "zh", "zl", "yh", "yl", "x"))
    data = ("zh", "zl", "yh", "yl", "x")
    placed = (
        P(None, data, None, None, None),
        P(None, data, None, None, None),
        P("section"),
        P("section", None),
        P("section", None, None),
        P("section", None, None),
    )
    return jax.shard_map(
        local,
        mesh=grid,
        in_specs=placed,
        out_specs=(P("section", None, None), P("section", None, None), P("section", None)),
        check_vma=False,
    )
```

```python
from functools import partial

import jax
import jax.numpy as jnp
from jax import lax
from jax.experimental import pallas as pl
from jax.experimental.pallas import tpu as pltpu
from jax.sharding import Mesh, PartitionSpec as P

EPSILON = 1e-06
f32, bf16 = jnp.float32, jnp.bfloat16
LANES = 128
QUARTERS = 4
NEAR = ("zl", "yl", "x")
FAR = ("zh", "yh")


def cells_kernel(
    where_, images, cotangent, vec_own, vec_far, point_own, point_far,
    kept, sent,
    point, vec, folded, packed, grads, opening, final,
    state_a, state_b, normed_a, normed_b, inverse_a, inverse_b, slope_a, slope_b, act_a, act_b,
    grad_act_a, grad_act_b, back_a, back_b, taps_a, taps_b, sems, out_sems,
):
    half, channels = point_own.shape[0], point_own.shape[2]
    slots = 2 * half
    block = channels // QUARTERS
    groups, height, width = images.shape[0], images.shape[2], images.shape[3]
    pixels = height * width
    share = groups // 2
    span = share * pixels
    tiles = channels // LANES
    state, normed, inverse = (state_a, state_b), (normed_a, normed_b), (inverse_a, inverse_b)
    slope, act, grad_act = (slope_a, slope_b), (act_a, act_b), (grad_act_a, grad_act_b)
    back, taps = (back_a, back_b), (taps_a, taps_b)

    mine = where_[0] * half
    theirs = half - mine
    def fetch(k):
        @pl.when(k // half == where_[0])
        def _():
            pltpu.make_async_copy(point_own.at[k % half], point.at[k], sems.at[k]).start()

        @pl.when(k // half != where_[0])
        def _():
            pltpu.make_async_copy(point_far.at[k % half], point.at[k], sems.at[k]).start()

    def arrived(k):
        pltpu.make_async_copy(point_own.at[0], point.at[k], sems.at[k]).wait()

    start = pltpu.make_async_copy(images.at[:, where_[0]], opening, sems.at[slots + 1])
    start.start()
    fetch(0)
    last = pltpu.make_async_copy(cotangent.at[:, where_[0]], final, sems.at[slots])
    for k in range(1, slots):
        fetch(k)
    last.start()
    for c in range(half):
        vec[mine + c] = vec_own[:, c, :]
        vec[theirs + c] = vec_far[:, c, :]
    count_own = jnp.max(vec_own[10, 0:1, :]).astype(jnp.int32)
    count_far = jnp.max(vec_far[10, 0:1, :]).astype(jnp.int32)
    first = jnp.where(where_[0] == 0, count_own, count_far)
    total = count_own + count_far

    def slot_of(i):
        return jnp.where(i < first, i, half + i - first)

    for k in range(slots):
        for t in range(9):
            folded[k, t:t + 1, :] = vec[k, t:t + 1, :] * vec[k, 9:10, :]
    start.wait()
    for m in range(groups):
        rows = slice(m % share * pixels, (m % share + 1) * pixels)
        state[m // share][rows] = opening[m].reshape(pixels, channels).astype(f32)

    column = lax.broadcasted_iota(jnp.int32, (width, LANES), 0)
    not_first = column > 0
    not_last = column < width - 1

    def from_left(a):
        return jnp.where(not_first, pltpu.roll(a, 1, 0), 0.0)

    def from_right(a):
        return jnp.where(not_last, pltpu.roll(a, width - 1, 0), 0.0)

    def rows_of(values):
        return [values[h * width:(h + 1) * width] for h in range(height)]

    def taps_of(k, cs):
        return [jnp.broadcast_to(folded[k, t:t + 1, cs], (width, LANES)) for t in range(9)]

    def convolve(k, s):
        for m in range(share):
            rows = slice(m * pixels, (m + 1) * pixels)
            x = state[s][rows, :]
            inv = lax.rsqrt(jnp.mean(x * x, axis=-1, keepdims=True) + EPSILON)
            inv = jnp.broadcast_to(inv, (pixels, LANES))
            inverse[s][k, rows, :] = inv
            for j in range(tiles):
                cs = slice(j * LANES, (j + 1) * LANES)
                xn = x[:, cs] * inv
                normed[s][k, rows, cs] = xn
                mid = rows_of(xn)
                src = ([from_left(a) for a in mid], mid, [from_right(a) for a in mid])
                w = taps_of(k, cs)
                acts, slopes = [], []
                for h in range(height):
                    lin = None
                    for p in range(3):
                        r = h + p - 1
                        if r < 0 or r >= height:
                            continue
                        for q in range(3):
                            term = w[p * 3 + q] * src[q][r]
                            lin = term if lin is None else lin + term
                    sig = 0.5 * jnp.tanh(0.5 * lin) + 0.5
                    a = lin * sig
                    acts.append(a)
                    slopes.append(sig + a * (1.0 - sig))
                act[s][k, rows, cs] = jnp.concatenate(acts, axis=0).astype(bf16)
                slope[s][k, rows, cs] = jnp.concatenate(slopes, axis=0)

    def project(k, s):
        for n in range(0, channels, 256):
            cs = slice(n, n + 256)
            mixed = jnp.dot(act[s][k], point[k, :, cs], preferred_element_type=f32)
            state[s][:, cs] = (state[s][:, cs] + mixed).astype(bf16).astype(f32)

    convolve(0, 0)

    def forward(i, carry):
        k = slot_of(i)
        arrived(k)
        project(k, 0)
        convolve(k, 1)
        project(k, 1)
        convolve(slot_of(i + 1), 0)
        return carry

    lax.fori_loop(0, total - 1, forward, 0)
    convolve(slot_of(total - 1), 1)
    arrived(slot_of(total - 1))
    last.wait()

    def pull_back(k, s, side):
        for n in range(0, channels, 256):
            cs = slice(n, n + 256)
            grad_act[s][:, cs] = lax.dot_general(
                grads[side, s * span:(s + 1) * span, :], point[k, cs, :],
                (((1,), (1,)), ((), ())), preferred_element_type=f32,
            )

    def unconvolve(k, s, side, onward=True):
        totals = [None] * share
        for j in range(tiles):
            cs = slice(j * LANES, (j + 1) * LANES)
            w = taps_of(k, cs)
            sums = [None] * 9
            for m in range(share):
                rows = slice(m * pixels, (m + 1) * pixels)
                gl = grad_act[s][rows, cs] * slope[s][k, rows, cs]
                xn = normed[s][k, rows, cs]
                xr = rows_of(xn)
                mid = rows_of(gl)
                src = ([from_right(a) for a in mid], mid, [from_left(a) for a in mid])
                us = []
                for h in range(height):
                    u = None
                    for p in range(3):
                        r = h - p + 1
                        if r < 0 or r >= height:
                            continue
                        for q in range(3):
                            t = p * 3 + q
                            if onward:
                                term = w[t] * src[q][r]
                                u = term if u is None else u + term
                            term = xr[h] * src[q][r]
                            sums[t] = term if sums[t] is None else sums[t] + term
                    us.append(u)
                if not onward:
                    continue
                u = jnp.concatenate(us, axis=0)
                back[s][rows, cs] = u
                totals[m] = u * xn if totals[m] is None else totals[m] + u * xn
            for t in range(9):
                taps[s][t * 8:(t + 1) * 8, cs] = sums[t]
        for m in range(share if onward else 0):
            rows = slice(m * pixels, (m + 1) * pixels)
            there = slice(s * span + m * pixels, s * span + (m + 1) * pixels)
            mean = jnp.sum(totals[m], axis=-1, keepdims=True) * (1.0 / channels)
            mean = jnp.broadcast_to(mean, (pixels, LANES))
            inv = inverse[s][k, rows, :]
            for j in range(tiles):
                cs = slice(j * LANES, (j + 1) * LANES)
                gx = inv * (back[s][rows, cs] - normed[s][k, rows, cs] * mean)
                gx = grads[side, there, cs].astype(f32) + gx
                grads[1 - side, there, cs] = gx.astype(bf16)

    def weigh(k, side):
        both = jnp.concatenate([act[0][k], act[1][k]], axis=0)
        g = grads[side]
        for r in range(QUARTERS):
            packed[QUARTERS * k + r, :block, :] = lax.dot_general(
                both[:, r * block:(r + 1) * block], g, (((0,), (0,)), ((), ())), preferred_element_type=f32
            ).astype(bf16)

    def summarise(k):
        gain = vec[k, 9:10, :]
        grad_gain = jnp.zeros((1, channels), f32)
        parts = []
        for t in range(9):
            both = taps[0][t * 8:(t + 1) * 8, :] + taps[1][t * 8:(t + 1) * 8, :]
            summed = jnp.sum(both, axis=0, keepdims=True)
            parts.append(summed * gain)
            grad_gain = grad_gain + vec[k, t:t + 1, :] * summed
        parts.append(grad_gain)
        for r in range(QUARTERS):
            some = parts[r * 3:r * 3 + 3]
            some = some + [jnp.zeros((8 - len(some), channels), f32)]
            packed[QUARTERS * k + r, block:block + 8, :] = jnp.concatenate(some, axis=0).astype(bf16)

    def send_out(k):
        cell = lax.rem(k, half)
        inside = packed.at[pl.ds(QUARTERS * k, QUARTERS)]
        outside = pl.ds(QUARTERS * cell, QUARTERS)

        @pl.when(lax.div(k, half) == where_[0])
        def _():
            pltpu.make_async_copy(inside, kept.at[outside], out_sems.at[k]).start()

        @pl.when(lax.div(k, half) != where_[0])
        def _():
            pltpu.make_async_copy(inside, sent.at[outside], out_sems.at[k]).start()

    for m in range(groups):
        grads[0, m * pixels:(m + 1) * pixels, :] = final[m].reshape(pixels, channels)
    pull_back(slot_of(total - 1), 0, 0)

    def backward(n, carry):
        i = total - 1 - n
        k = slot_of(i)
        side = lax.rem(n, 2)
        pull_back(k, 1, side)
        unconvolve(k, 0, side)
        weigh(k, side)
        pull_back(slot_of(i - 1), 0, 1 - side)
        unconvolve(k, 1, side)
        summarise(k)
        send_out(k)
        return carry

    lax.fori_loop(0, total - 1, backward, 0)
    side = lax.rem(total - 1, 2)
    pull_back(0, 1, side)
    unconvolve(0, 0, side, False)
    weigh(0, side)
    unconvolve(0, 1, side, False)
    summarise(0)
    send_out(0)

    def idle(k, carry):
        @pl.when(lax.rem(k, half) >= jnp.where(k < half, first, total - first))
        def _():
            arrived(k)
            packed[pl.ds(QUARTERS * k, QUARTERS)] = jnp.zeros((QUARTERS, block + 8, channels), bf16)
            send_out(k)
        return carry

    lax.fori_loop(0, slots, idle, 0)
    for k in range(slots):
        pltpu.make_async_copy(
            packed.at[QUARTERS * k:QUARTERS * (k + 1)], kept.at[0:QUARTERS], out_sems.at[k]
        ).wait()


def run_cells(section, images, cotangent, vec_own, vec_far, point_own, point_far):
    half = point_own.shape[0]
    slots = 2 * half
    groups, unused, height, width, channels = images.shape
    total = groups * height * width
    span = total // 2
    out = jax.ShapeDtypeStruct((QUARTERS * half, channels // QUARTERS + 8, channels), bf16)

    def pair(shape, dtype):
        return [pltpu.VMEM(shape, dtype)] * 2

    spec = pltpu.PrefetchScalarGridSpec(
        num_scalar_prefetch=1,
        grid=(1,),
        in_specs=[
            pl.BlockSpec(memory_space=pltpu.HBM),
            pl.BlockSpec(memory_space=pltpu.HBM),
            pl.BlockSpec(vec_own.shape, lambda i, s: (0, 0, 0)),
            pl.BlockSpec(vec_far.shape, lambda i, s: (0, 0, 0)),
            pl.BlockSpec(memory_space=pltpu.HBM),
            pl.BlockSpec(memory_space=pl.ANY),
        ],
        out_specs=[pl.BlockSpec(memory_space=pl.ANY)] * 2,
        scratch_shapes=[
            pltpu.VMEM((slots, channels, channels), bf16),
            pltpu.VMEM((slots, 11, channels), f32),
            pltpu.VMEM((slots, 9, channels), f32),
            pltpu.VMEM((QUARTERS * slots, channels // QUARTERS + 8, channels), bf16),
            pltpu.VMEM((2, total, channels), bf16),
            pltpu.VMEM((groups, height, width, channels), bf16),
            pltpu.VMEM((groups, height, width, channels), bf16),
            *pair((span, channels), f32),
            *pair((slots, span, channels), f32),
            *pair((slots, span, LANES), f32),
            *pair((slots, span, channels), f32),
            *pair((slots, span, channels), bf16),
            *pair((span, channels), f32),
            *pair((span, channels), f32),
            *pair((72, channels), f32),
            pltpu.SemaphoreType.DMA((slots + 2,)),
            pltpu.SemaphoreType.DMA((slots,)),
        ],
    )
    return pl.pallas_call(
        cells_kernel,
        grid_spec=spec,
        out_shape=[out, out],
        compiler_params=pltpu.CompilerParams(vmem_limit_bytes=26 << 20),
        name="cells",
    )(section, images, cotangent, vec_own, vec_far, point_own, point_far)


def swapped(block):
    return lax.ppermute(block, "section", [(0, 1), (1, 0)])


def exchanged(block, axes):
    return lax.all_to_all(block, axes, 0, 0, tiled=True)


def added(blocks):
    return jnp.sum(blocks.astype(f32), axis=0)


def local(images, cotangent, counts, gains, depthwise, pointwise):
    cells, channels = gains.shape
    section = lax.axis_index("section").astype(jnp.int32)
    point_far = swapped(pointwise)
    vec_own = jnp.concatenate(
        [
            jnp.transpose(depthwise, (1, 0, 2)),
            gains[None],
            jnp.broadcast_to(counts.astype(f32)[:, None, None], (1, cells, channels)),
        ],
        axis=0,
    )
    vec_far = swapped(vec_own)
    images, cotangent, pointwise = (
        pltpu.with_memory_space_constraint(a, pltpu.HBM) for a in (images, cotangent, pointwise)
    )
    kept, sent = run_cells(section[None], images, cotangent, vec_own, vec_far, pointwise, point_far)
    summed = (kept.astype(f32) + swapped(sent).astype(f32)).astype(bf16)

    near, rows, unused = summed.shape
    rows -= 8
    far = lax.axis_size(FAR)
    part = added(exchanged(summed, NEAR))
    strip = part[rows:rows + 4].reshape(-1, LANES)
    strip = jnp.pad(strip, ((0, rows - strip.shape[0]), (0, 0)))
    wide = jnp.concatenate([part[:rows], strip], axis=1).astype(bf16).reshape(far, rows // far, channels + LANES)
    piece = added(exchanged(wide, FAR)).astype(bf16)

    back = exchanged(jnp.broadcast_to(piece, wide.shape), FAR).reshape(rows, channels + LANES)
    small = back[:32, channels:].reshape(8, channels)
    back = jnp.concatenate([back[:, :channels], small], axis=0)
    out = exchanged(jnp.broadcast_to(back, summed.shape), NEAR).astype(f32)
    small = out[:, rows:rows + 3].reshape(cells, 3 * QUARTERS, channels)
    return out[:, :rows].reshape(cells, channels, channels), small[:, :9], small[:, 9]


def solution(mesh):
    grid = Mesh(mesh.devices.reshape(2, 4, 2, 4, 2, 4), ("section", "zh", "zl", "yh", "yl", "x"))
    data = ("zh", "zl", "yh", "yl", "x")
    placed = (
        P(None, data, None, None, None),
        P(None, data, None, None, None),
        P("section"),
        P("section", None),
        P("section", None, None),
        P("section", None, None),
    )
    return jax.shard_map(
        local,
        mesh=grid,
        in_specs=placed,
        out_specs=(P("section", None, None), P("section", None, None), P("section", None)),
        check_vma=False,
    )
```

```python
from functools import partial

import jax
import jax.numpy as jnp
from jax import lax
from jax.experimental import pallas as pl
from jax.experimental.pallas import tpu as pltpu
from jax.sharding import Mesh, PartitionSpec as P

EPSILON = 1e-06
f32, bf16 = jnp.float32, jnp.bfloat16
LANES = 128
QUARTERS = 4
NEAR = ("zl", "yl", "x")
FAR = ("zh", "yh")


def cells_kernel(
    where_, images, cotangent, vec_own, vec_far, point_own, point_far,
    kept, sent,
    point, vec, folded, packed, grads, opening, final,
    state_a, state_b, normed_a, normed_b, inverse_a, inverse_b, slope_a, slope_b, act_a, act_b,
    grad_act_a, grad_act_b, back_a, back_b, taps_a, taps_b, sems, out_sems,
):
    half, channels = point_own.shape[0], point_own.shape[2]
    slots = 2 * half
    block = channels // QUARTERS
    groups, height, width = images.shape[0], images.shape[2], images.shape[3]
    pixels = height * width
    share = groups // 2
    span = share * pixels
    tiles = channels // LANES
    state, normed, inverse = (state_a, state_b), (normed_a, normed_b), (inverse_a, inverse_b)
    slope, act, grad_act = (slope_a, slope_b), (act_a, act_b), (grad_act_a, grad_act_b)
    back, taps = (back_a, back_b), (taps_a, taps_b)

    mine = where_[0] * half
    theirs = half - mine
    def fetch(k):
        @pl.when(k // half == where_[0])
        def _():
            pltpu.make_async_copy(point_own.at[k % half], point.at[k], sems.at[k]).start()

        @pl.when(k // half != where_[0])
        def _():
            pltpu.make_async_copy(point_far.at[k % half], point.at[k], sems.at[k]).start()

    def arrived(k):
        pltpu.make_async_copy(point_own.at[0], point.at[k], sems.at[k]).wait()

    start = pltpu.make_async_copy(images.at[:, where_[0]], opening, sems.at[slots + 1])
    start.start()
    fetch(0)
    last = pltpu.make_async_copy(cotangent.at[:, where_[0]], final, sems.at[slots])
    for k in range(1, slots):
        fetch(k)
    last.start()
    for c in range(half):
        vec[mine + c] = vec_own[:, c, :]
        vec[theirs + c] = vec_far[:, c, :]
    count_own = jnp.max(vec_own[10, 0:1, :]).astype(jnp.int32)
    count_far = jnp.max(vec_far[10, 0:1, :]).astype(jnp.int32)
    first = jnp.where(where_[0] == 0, count_own, count_far)
    total = count_own + count_far

    def slot_of(i):
        return jnp.where(i < first, i, half + i - first)

    for k in range(slots):
        for t in range(9):
            folded[k, t:t + 1, :] = vec[k, t:t + 1, :] * vec[k, 9:10, :]
    start.wait()
    for m in range(groups):
        rows = slice(m % share * pixels, (m % share + 1) * pixels)
        state[m // share][rows] = opening[m].reshape(pixels, channels).astype(f32)

    column = lax.broadcasted_iota(jnp.int32, (width, LANES), 0)
    not_first = column > 0
    not_last = column < width - 1

    def from_left(a):
        return jnp.where(not_first, pltpu.roll(a, 1, 0), 0.0)

    def from_right(a):
        return jnp.where(not_last, pltpu.roll(a, width - 1, 0), 0.0)

    def rows_of(values):
        return [values[h * width:(h + 1) * width] for h in range(height)]

    def taps_of(k, cs):
        return [jnp.broadcast_to(folded[k, t:t + 1, cs], (width, LANES)) for t in range(9)]

    def convolve(k, s):
        for m in range(share):
            rows = slice(m * pixels, (m + 1) * pixels)
            x = state[s][rows, :]
            inv = lax.rsqrt(jnp.mean(x * x, axis=-1, keepdims=True) + EPSILON)
            inv = jnp.broadcast_to(inv, (pixels, LANES))
            inverse[s][k, rows, :] = inv
            for j in range(tiles):
                cs = slice(j * LANES, (j + 1) * LANES)
                xn = x[:, cs] * inv
                normed[s][k, rows, cs] = xn
                mid = rows_of(xn)
                src = ([from_left(a) for a in mid], mid, [from_right(a) for a in mid])
                w = taps_of(k, cs)
                acts, slopes = [], []
                for h in range(height):
                    lin = None
                    for p in range(3):
                        r = h + p - 1
                        if r < 0 or r >= height:
                            continue
                        for q in range(3):
                            term = w[p * 3 + q] * src[q][r]
                            lin = term if lin is None else lin + term
                    sig = 0.5 * jnp.tanh(0.5 * lin) + 0.5
                    a = lin * sig
                    acts.append(a)
                    slopes.append(sig + a * (1.0 - sig))
                act[s][k, rows, cs] = jnp.concatenate(acts, axis=0).astype(bf16)
                slope[s][k, rows, cs] = jnp.concatenate(slopes, axis=0)

    def project(k, s):
        for n in range(0, channels, 256):
            cs = slice(n, n + 256)
            mixed = jnp.dot(act[s][k], point[k, :, cs], preferred_element_type=f32)
            state[s][:, cs] = (state[s][:, cs] + mixed).astype(bf16).astype(f32)

    convolve(0, 0)

    def forward(i, carry):
        k = slot_of(i)
        arrived(k)
        project(k, 0)
        convolve(k, 1)
        project(k, 1)
        convolve(slot_of(i + 1), 0)
        return carry

    lax.fori_loop(0, total - 1, forward, 0)
    convolve(slot_of(total - 1), 1)
    arrived(slot_of(total - 1))
    last.wait()

    def pull_back(k, s, side):
        for n in range(0, channels, 256):
            cs = slice(n, n + 256)
            grad_act[s][:, cs] = lax.dot_general(
                grads[side, s * span:(s + 1) * span, :], point[k, cs, :],
                (((1,), (1,)), ((), ())), preferred_element_type=f32,
            )

    def unconvolve(k, s, side, onward=True):
        totals = [None] * share
        for j in range(tiles):
            cs = slice(j * LANES, (j + 1) * LANES)
            w = taps_of(k, cs)
            sums = [None] * 9
            for m in range(share):
                rows = slice(m * pixels, (m + 1) * pixels)
                gl = grad_act[s][rows, cs] * slope[s][k, rows, cs]
                xn = normed[s][k, rows, cs]
                xr = rows_of(xn)
                mid = rows_of(gl)
                src = ([from_right(a) for a in mid], mid, [from_left(a) for a in mid])
                us = []
                for h in range(height):
                    u = None
                    for p in range(3):
                        r = h - p + 1
                        if r < 0 or r >= height:
                            continue
                        for q in range(3):
                            t = p * 3 + q
                            if onward:
                                term = w[t] * src[q][r]
                                u = term if u is None else u + term
                            term = xr[h] * src[q][r]
                            sums[t] = term if sums[t] is None else sums[t] + term
                    us.append(u)
                if not onward:
                    continue
                u = jnp.concatenate(us, axis=0)
                back[s][rows, cs] = u
                totals[m] = u * xn if totals[m] is None else totals[m] + u * xn
            for t in range(9):
                taps[s][t * 8:(t + 1) * 8, cs] = sums[t]
        for m in range(share if onward else 0):
            rows = slice(m * pixels, (m + 1) * pixels)
            there = slice(s * span + m * pixels, s * span + (m + 1) * pixels)
            mean = jnp.sum(totals[m], axis=-1, keepdims=True) * (1.0 / channels)
            mean = jnp.broadcast_to(mean, (pixels, LANES))
            inv = inverse[s][k, rows, :]
            for j in range(tiles):
                cs = slice(j * LANES, (j + 1) * LANES)
                gx = inv * (back[s][rows, cs] - normed[s][k, rows, cs] * mean)
                gx = grads[side, there, cs].astype(f32) + gx
                grads[1 - side, there, cs] = gx.astype(bf16)

    def weigh(k, side):
        both = jnp.concatenate([act[0][k], act[1][k]], axis=0)
        g = grads[side]
        for r in range(QUARTERS):
            packed[QUARTERS * k + r, :block, :] = lax.dot_general(
                both[:, r * block:(r + 1) * block], g, (((0,), (0,)), ((), ())), preferred_element_type=f32
            ).astype(bf16)

    def summarise(k):
        gain = vec[k, 9:10, :]
        grad_gain = jnp.zeros((1, channels), f32)
        parts = []
        for t in range(9):
            both = taps[0][t * 8:(t + 1) * 8, :] + taps[1][t * 8:(t + 1) * 8, :]
            summed = jnp.sum(both, axis=0, keepdims=True)
            parts.append(summed * gain)
            grad_gain = grad_gain + vec[k, t:t + 1, :] * summed
        parts.append(grad_gain)
        for r in range(QUARTERS):
            some = parts[r * 3:r * 3 + 3]
            some = some + [jnp.zeros((8 - len(some), channels), f32)]
            packed[QUARTERS * k + r, block:block + 8, :] = jnp.concatenate(some, axis=0).astype(bf16)

    def send_out(k):
        cell = lax.rem(k, half)
        inside = packed.at[pl.ds(QUARTERS * k, QUARTERS)]
        outside = pl.ds(QUARTERS * cell, QUARTERS)

        @pl.when(lax.div(k, half) == where_[0])
        def _():
            pltpu.make_async_copy(inside, kept.at[outside], out_sems.at[k]).start()

        @pl.when(lax.div(k, half) != where_[0])
        def _():
            pltpu.make_async_copy(inside, sent.at[outside], out_sems.at[k]).start()

    for m in range(groups):
        grads[0, m * pixels:(m + 1) * pixels, :] = final[m].reshape(pixels, channels)
    pull_back(slot_of(total - 1), 0, 0)

    def backward(n, carry):
        i = total - 1 - n
        k = slot_of(i)
        side = lax.rem(n, 2)
        pull_back(k, 1, side)
        unconvolve(k, 0, side)
        weigh(k, side)
        pull_back(slot_of(i - 1), 0, 1 - side)
        unconvolve(k, 1, side)
        summarise(k)
        send_out(k)
        return carry

    lax.fori_loop(0, total - 1, backward, 0)
    side = lax.rem(total - 1, 2)
    pull_back(0, 1, side)
    unconvolve(0, 0, side, False)
    weigh(0, side)
    unconvolve(0, 1, side, False)
    summarise(0)
    send_out(0)

    def idle(k, carry):
        @pl.when(lax.rem(k, half) >= jnp.where(k < half, first, total - first))
        def _():
            arrived(k)
            packed[pl.ds(QUARTERS * k, QUARTERS)] = jnp.zeros((QUARTERS, block + 8, channels), bf16)
            send_out(k)
        return carry

    lax.fori_loop(0, slots, idle, 0)
    for k in range(slots):
        pltpu.make_async_copy(
            packed.at[QUARTERS * k:QUARTERS * (k + 1)], kept.at[0:QUARTERS], out_sems.at[k]
        ).wait()


def run_cells(section, images, cotangent, vec_own, vec_far, point_own, point_far):
    half = point_own.shape[0]
    slots = 2 * half
    groups, unused, height, width, channels = images.shape
    total = groups * height * width
    span = total // 2
    out = jax.ShapeDtypeStruct((QUARTERS * half, channels // QUARTERS + 8, channels), bf16)

    def pair(shape, dtype):
        return [pltpu.VMEM(shape, dtype)] * 2

    spec = pltpu.PrefetchScalarGridSpec(
        num_scalar_prefetch=1,
        grid=(1,),
        in_specs=[
            pl.BlockSpec(memory_space=pltpu.HBM),
            pl.BlockSpec(memory_space=pltpu.HBM),
            pl.BlockSpec(vec_own.shape, lambda i, s: (0, 0, 0)),
            pl.BlockSpec(vec_far.shape, lambda i, s: (0, 0, 0)),
            pl.BlockSpec(memory_space=pltpu.HBM),
            pl.BlockSpec(memory_space=pl.ANY),
        ],
        out_specs=[pl.BlockSpec(memory_space=pl.ANY)] * 2,
        scratch_shapes=[
            pltpu.VMEM((slots, channels, channels), bf16),
            pltpu.VMEM((slots, 11, channels), f32),
            pltpu.VMEM((slots, 9, channels), f32),
            pltpu.VMEM((QUARTERS * slots, channels // QUARTERS + 8, channels), bf16),
            pltpu.VMEM((2, total, channels), bf16),
            pltpu.VMEM((groups, height, width, channels), bf16),
            pltpu.VMEM((groups, height, width, channels), bf16),
            *pair((span, channels), f32),
            *pair((slots, span, channels), f32),
            *pair((slots, span, LANES), f32),
            *pair((slots, span, channels), f32),
            *pair((slots, span, channels), bf16),
            *pair((span, channels), f32),
            *pair((span, channels), f32),
            *pair((72, channels), f32),
            pltpu.SemaphoreType.DMA((slots + 2,)),
            pltpu.SemaphoreType.DMA((slots,)),
        ],
    )
    return pl.pallas_call(
        cells_kernel,
        grid_spec=spec,
        out_shape=[out, out],
        compiler_params=pltpu.CompilerParams(vmem_limit_bytes=26 << 20),
        name="cells",
    )(section, images, cotangent, vec_own, vec_far, point_own, point_far)


def widen_kernel(totals, grad_point, grad_depth, grad_gain, wide, sems):
    count, rows = wide.shape[0], wide.shape[1]
    copies = []
    for n in range(count):
        wide[n] = totals[n, :rows, :].astype(f32)
        where = grad_point.at[n // QUARTERS, pl.ds(n % QUARTERS * rows, rows)]
        copies.append(pltpu.make_async_copy(wide.at[n], where, sems.at[n]))
        copies[n].start()
    for n in range(count):
        cell, r = n // QUARTERS, n % QUARTERS
        some = totals[n, rows:rows + 8, :].astype(f32)
        for i in range(3):
            t = 3 * r + i
            if t < 9:
                grad_depth[t, cell:cell + 1, :] = some[i:i + 1]
            elif t == 9:
                grad_gain[cell:cell + 1, :] = some[i:i + 1]
    for copy in copies:
        copy.wait()


def widened(totals, cells, channels):
    count, rows = totals.shape[0], totals.shape[1] - 8
    return pl.pallas_call(
        widen_kernel,
        in_specs=[pl.BlockSpec(memory_space=pltpu.VMEM)],
        out_specs=[pl.BlockSpec(memory_space=pl.ANY)] + [pl.BlockSpec(memory_space=pltpu.VMEM)] * 2,
        out_shape=[
            jax.ShapeDtypeStruct((cells, channels, channels), f32),
            jax.ShapeDtypeStruct((9, cells, channels), f32),
            jax.ShapeDtypeStruct((cells, channels), f32),
        ],
        scratch_shapes=[pltpu.VMEM((count, rows, channels), f32), pltpu.SemaphoreType.DMA((count,))],
        compiler_params=pltpu.CompilerParams(vmem_limit_bytes=12 << 20),
        name="widen",
    )(totals)


def swapped(block):
    return lax.ppermute(block, "section", [(0, 1), (1, 0)])


def exchanged(block, axes):
    return lax.all_to_all(block, axes, 0, 0, tiled=True)


def added(blocks):
    return jnp.sum(blocks.astype(f32), axis=0)


def local(images, cotangent, counts, gains, depthwise, pointwise):
    cells, channels = gains.shape
    section = lax.axis_index("section").astype(jnp.int32)
    point_far = swapped(pointwise)
    vec_own = jnp.concatenate(
        [
            jnp.transpose(depthwise, (1, 0, 2)),
            gains[None],
            jnp.broadcast_to(counts.astype(f32)[:, None, None], (1, cells, channels)),
        ],
        axis=0,
    )
    vec_far = swapped(vec_own)
    images, cotangent, pointwise = (
        pltpu.with_memory_space_constraint(a, pltpu.HBM) for a in (images, cotangent, pointwise)
    )
    kept, sent = run_cells(section[None], images, cotangent, vec_own, vec_far, pointwise, point_far)
    summed = (kept.astype(f32) + swapped(sent).astype(f32)).astype(bf16)

    near, rows, unused = summed.shape
    rows -= 8
    far = lax.axis_size(FAR)
    part = added(exchanged(summed, NEAR))
    strip = part[rows:rows + 4].reshape(-1, LANES)
    strip = jnp.pad(strip, ((0, rows - strip.shape[0]), (0, 0)))
    wide = jnp.concatenate([part[:rows], strip], axis=1).astype(bf16).reshape(far, rows // far, channels + LANES)
    piece = added(exchanged(wide, FAR)).astype(bf16)

    back = exchanged(jnp.broadcast_to(piece, wide.shape), FAR).reshape(rows, channels + LANES)
    small = back[:32, channels:].reshape(8, channels)
    back = jnp.concatenate([back[:, :channels], small], axis=0)
    out = exchanged(jnp.broadcast_to(back, summed.shape), NEAR)
    grad_point, grad_depth, grad_gain = widened(out, cells, channels)
    return grad_point, jnp.transpose(grad_depth, (1, 0, 2)), grad_gain


def solution(mesh):
    grid = Mesh(mesh.devices.reshape(2, 4, 2, 4, 2, 4), ("section", "zh", "zl", "yh", "yl", "x"))
    data = ("zh", "zl", "yh", "yl", "x")
    placed = (
        P(None, data, None, None, None),
        P(None, data, None, None, None),
        P("section"),
        P("section", None),
        P("section", None, None),
        P("section", None, None),
    )
    return jax.shard_map(
        local,
        mesh=grid,
        in_specs=placed,
        out_specs=(P("section", None, None), P("section", None, None), P("section", None)),
        check_vma=False,
    )
```

```python
from functools import partial

import jax
import jax.numpy as jnp
from jax import lax
from jax.experimental import pallas as pl
from jax.experimental.pallas import tpu as pltpu
from jax.sharding import Mesh, PartitionSpec as P

EPSILON = 1e-06
f32, bf16 = jnp.float32, jnp.bfloat16
LANES = 128
QUARTERS = 4
NEAR = ("yl", "x", "zl")
FAR = ("zh", "yh")


def cells_kernel(
    where_, images, cotangent, vec_own, vec_far, point_own, point_far,
    kept, sent,
    point, vec, folded, packed, grads, opening, final,
    state_a, state_b, normed_a, normed_b, inverse_a, inverse_b, slope_a, slope_b, act_a, act_b,
    grad_act_a, grad_act_b, back_a, back_b, taps_a, taps_b, sems, out_sems,
):
    half, channels = point_own.shape[0], point_own.shape[2]
    slots = 2 * half
    block = channels // QUARTERS
    groups, height, width = images.shape[0], images.shape[2], images.shape[3]
    pixels = height * width
    share = groups // 2
    span = share * pixels
    tiles = channels // LANES
    state, normed, inverse = (state_a, state_b), (normed_a, normed_b), (inverse_a, inverse_b)
    slope, act, grad_act = (slope_a, slope_b), (act_a, act_b), (grad_act_a, grad_act_b)
    back, taps = (back_a, back_b), (taps_a, taps_b)

    mine = where_[0] * half
    theirs = half - mine
    def fetch(k):
        @pl.when(k // half == where_[0])
        def _():
            pltpu.make_async_copy(point_own.at[k % half], point.at[k], sems.at[k]).start()

        @pl.when(k // half != where_[0])
        def _():
            pltpu.make_async_copy(point_far.at[k % half], point.at[k], sems.at[k]).start()

    def arrived(k):
        pltpu.make_async_copy(point_own.at[0], point.at[k], sems.at[k]).wait()

    start = pltpu.make_async_copy(images.at[:, where_[0]], opening, sems.at[slots + 1])
    start.start()
    fetch(0)
    last = pltpu.make_async_copy(cotangent.at[:, where_[0]], final, sems.at[slots])
    for k in range(1, slots):
        fetch(k)
    last.start()
    for c in range(half):
        vec[mine + c] = vec_own[:, c, :]
        vec[theirs + c] = vec_far[:, c, :]
    count_own = jnp.max(vec_own[10, 0:1, :]).astype(jnp.int32)
    count_far = jnp.max(vec_far[10, 0:1, :]).astype(jnp.int32)
    first = jnp.where(where_[0] == 0, count_own, count_far)
    total = count_own + count_far

    def slot_of(i):
        return jnp.where(i < first, i, half + i - first)

    for k in range(slots):
        for t in range(9):
            folded[k, t:t + 1, :] = vec[k, t:t + 1, :] * vec[k, 9:10, :]
    start.wait()
    for m in range(groups):
        rows = slice(m % share * pixels, (m % share + 1) * pixels)
        state[m // share][rows] = opening[m].reshape(pixels, channels).astype(f32)

    column = lax.broadcasted_iota(jnp.int32, (width, LANES), 0)
    not_first = column > 0
    not_last = column < width - 1

    def from_left(a):
        return jnp.where(not_first, pltpu.roll(a, 1, 0), 0.0)

    def from_right(a):
        return jnp.where(not_last, pltpu.roll(a, width - 1, 0), 0.0)

    def rows_of(values):
        return [values[h * width:(h + 1) * width] for h in range(height)]

    def taps_of(k, cs):
        return [jnp.broadcast_to(folded[k, t:t + 1, cs], (width, LANES)) for t in range(9)]

    def convolve(k, s):
        for m in range(share):
            rows = slice(m * pixels, (m + 1) * pixels)
            x = state[s][rows, :]
            inv = lax.rsqrt(jnp.mean(x * x, axis=-1, keepdims=True) + EPSILON)
            inv = jnp.broadcast_to(inv, (pixels, LANES))
            inverse[s][k, rows, :] = inv
            for j in range(tiles):
                cs = slice(j * LANES, (j + 1) * LANES)
                xn = x[:, cs] * inv
                normed[s][k, rows, cs] = xn
                mid = rows_of(xn)
                src = ([from_left(a) for a in mid], mid, [from_right(a) for a in mid])
                w = taps_of(k, cs)
                acts, slopes = [], []
                for h in range(height):
                    lin = None
                    for p in range(3):
                        r = h + p - 1
                        if r < 0 or r >= height:
                            continue
                        for q in range(3):
                            term = w[p * 3 + q] * src[q][r]
                            lin = term if lin is None else lin + term
                    sig = 0.5 * jnp.tanh(0.5 * lin) + 0.5
                    a = lin * sig
                    acts.append(a)
                    slopes.append(sig + a * (1.0 - sig))
                act[s][k, rows, cs] = jnp.concatenate(acts, axis=0).astype(bf16)
                slope[s][k, rows, cs] = jnp.concatenate(slopes, axis=0)

    def project(k, s):
        for n in range(0, channels, 256):
            cs = slice(n, n + 256)
            mixed = jnp.dot(act[s][k], point[k, :, cs], preferred_element_type=f32)
            state[s][:, cs] = (state[s][:, cs] + mixed).astype(bf16).astype(f32)

    convolve(0, 0)

    def forward(i, carry):
        k = slot_of(i)
        arrived(k)
        project(k, 0)
        convolve(k, 1)
        project(k, 1)
        convolve(slot_of(i + 1), 0)
        return carry

    lax.fori_loop(0, total - 1, forward, 0)
    convolve(slot_of(total - 1), 1)
    arrived(slot_of(total - 1))
    last.wait()

    def pull_back(k, s, side):
        for n in range(0, channels, 256):
            cs = slice(n, n + 256)
            grad_act[s][:, cs] = lax.dot_general(
                grads[side, s * span:(s + 1) * span, :], point[k, cs, :],
                (((1,), (1,)), ((), ())), preferred_element_type=f32,
            )

    def unconvolve(k, s, side, onward=True):
        totals = [None] * share
        for j in range(tiles):
            cs = slice(j * LANES, (j + 1) * LANES)
            w = taps_of(k, cs)
            sums = [None] * 9
            for m in range(share):
                rows = slice(m * pixels, (m + 1) * pixels)
                gl = grad_act[s][rows, cs] * slope[s][k, rows, cs]
                xn = normed[s][k, rows, cs]
                xr = rows_of(xn)
                mid = rows_of(gl)
                src = ([from_right(a) for a in mid], mid, [from_left(a) for a in mid])
                us = []
                for h in range(height):
                    u = None
                    for p in range(3):
                        r = h - p + 1
                        if r < 0 or r >= height:
                            continue
                        for q in range(3):
                            t = p * 3 + q
                            if onward:
                                term = w[t] * src[q][r]
                                u = term if u is None else u + term
                            term = xr[h] * src[q][r]
                            sums[t] = term if sums[t] is None else sums[t] + term
                    us.append(u)
                if not onward:
                    continue
                u = jnp.concatenate(us, axis=0)
                back[s][rows, cs] = u
                totals[m] = u * xn if totals[m] is None else totals[m] + u * xn
            for t in range(9):
                taps[s][t * 8:(t + 1) * 8, cs] = sums[t]
        for m in range(share if onward else 0):
            rows = slice(m * pixels, (m + 1) * pixels)
            there = slice(s * span + m * pixels, s * span + (m + 1) * pixels)
            mean = jnp.sum(totals[m], axis=-1, keepdims=True) * (1.0 / channels)
            mean = jnp.broadcast_to(mean, (pixels, LANES))
            inv = inverse[s][k, rows, :]
            for j in range(tiles):
                cs = slice(j * LANES, (j + 1) * LANES)
                gx = inv * (back[s][rows, cs] - normed[s][k, rows, cs] * mean)
                gx = grads[side, there, cs].astype(f32) + gx
                grads[1 - side, there, cs] = gx.astype(bf16)

    def weigh(k, side):
        both = jnp.concatenate([act[0][k], act[1][k]], axis=0)
        g = grads[side]
        for r in range(QUARTERS):
            packed[QUARTERS * k + r, :block, :] = lax.dot_general(
                both[:, r * block:(r + 1) * block], g, (((0,), (0,)), ((), ())), preferred_element_type=f32
            ).astype(bf16)

    def summarise(k):
        gain = vec[k, 9:10, :]
        grad_gain = jnp.zeros((1, channels), f32)
        parts = []
        for t in range(9):
            both = taps[0][t * 8:(t + 1) * 8, :] + taps[1][t * 8:(t + 1) * 8, :]
            summed = jnp.sum(both, axis=0, keepdims=True)
            parts.append(summed * gain)
            grad_gain = grad_gain + vec[k, t:t + 1, :] * summed
        parts.append(grad_gain)
        for r in range(QUARTERS):
            some = parts[r * 3:r * 3 + 3]
            some = some + [jnp.zeros((8 - len(some), channels), f32)]
            packed[QUARTERS * k + r, block:block + 8, :] = jnp.concatenate(some, axis=0).astype(bf16)

    def send_out(k):
        cell = lax.rem(k, half)
        inside = packed.at[pl.ds(QUARTERS * k, QUARTERS)]
        outside = pl.ds(QUARTERS * cell, QUARTERS)

        @pl.when(lax.div(k, half) == where_[0])
        def _():
            pltpu.make_async_copy(inside, kept.at[outside], out_sems.at[k]).start()

        @pl.when(lax.div(k, half) != where_[0])
        def _():
            pltpu.make_async_copy(inside, sent.at[outside], out_sems.at[k]).start()

    for m in range(groups):
        grads[0, m * pixels:(m + 1) * pixels, :] = final[m].reshape(pixels, channels)
    pull_back(slot_of(total - 1), 0, 0)

    def backward(n, carry):
        i = total - 1 - n
        k = slot_of(i)
        side = lax.rem(n, 2)
        pull_back(k, 1, side)
        unconvolve(k, 0, side)
        weigh(k, side)
        pull_back(slot_of(i - 1), 0, 1 - side)
        unconvolve(k, 1, side)
        summarise(k)
        send_out(k)
        return carry

    lax.fori_loop(0, total - 1, backward, 0)
    side = lax.rem(total - 1, 2)
    pull_back(0, 1, side)
    unconvolve(0, 0, side, False)
    weigh(0, side)
    unconvolve(0, 1, side, False)
    summarise(0)
    send_out(0)

    def idle(k, carry):
        @pl.when(lax.rem(k, half) >= jnp.where(k < half, first, total - first))
        def _():
            arrived(k)
            packed[pl.ds(QUARTERS * k, QUARTERS)] = jnp.zeros((QUARTERS, block + 8, channels), bf16)
            send_out(k)
        return carry

    lax.fori_loop(0, slots, idle, 0)
    for k in range(slots):
        pltpu.make_async_copy(
            packed.at[QUARTERS * k:QUARTERS * (k + 1)], kept.at[0:QUARTERS], out_sems.at[k]
        ).wait()


def run_cells(section, images, cotangent, vec_own, vec_far, point_own, point_far):
    half = point_own.shape[0]
    slots = 2 * half
    groups, unused, height, width, channels = images.shape
    total = groups * height * width
    span = total // 2
    out = jax.ShapeDtypeStruct((QUARTERS * half, channels // QUARTERS + 8, channels), bf16)

    def pair(shape, dtype):
        return [pltpu.VMEM(shape, dtype)] * 2

    spec = pltpu.PrefetchScalarGridSpec(
        num_scalar_prefetch=1,
        grid=(1,),
        in_specs=[
            pl.BlockSpec(memory_space=pltpu.HBM),
            pl.BlockSpec(memory_space=pltpu.HBM),
            pl.BlockSpec(vec_own.shape, lambda i, s: (0, 0, 0)),
            pl.BlockSpec(vec_far.shape, lambda i, s: (0, 0, 0)),
            pl.BlockSpec(memory_space=pltpu.HBM),
            pl.BlockSpec(memory_space=pl.ANY),
        ],
        out_specs=[pl.BlockSpec(memory_space=pl.ANY)] * 2,
        scratch_shapes=[
            pltpu.VMEM((slots, channels, channels), bf16),
            pltpu.VMEM((slots, 11, channels), f32),
            pltpu.VMEM((slots, 9, channels), f32),
            pltpu.VMEM((QUARTERS * slots, channels // QUARTERS + 8, channels), bf16),
            pltpu.VMEM((2, total, channels), bf16),
            pltpu.VMEM((groups, height, width, channels), bf16),
            pltpu.VMEM((groups, height, width, channels), bf16),
            *pair((span, channels), f32),
            *pair((slots, span, channels), f32),
            *pair((slots, span, LANES), f32),
            *pair((slots, span, channels), f32),
            *pair((slots, span, channels), bf16),
            *pair((span, channels), f32),
            *pair((span, channels), f32),
            *pair((72, channels), f32),
            pltpu.SemaphoreType.DMA((slots + 2,)),
            pltpu.SemaphoreType.DMA((slots,)),
        ],
    )
    return pl.pallas_call(
        cells_kernel,
        grid_spec=spec,
        out_shape=[out, out],
        compiler_params=pltpu.CompilerParams(vmem_limit_bytes=26 << 20),
        name="cells",
    )(section, images, cotangent, vec_own, vec_far, point_own, point_far)


def widen_kernel(totals, grad_point, grad_depth, grad_gain, wide, sems):
    count, rows = wide.shape[0], wide.shape[1]
    copies = []
    for n in range(count):
        wide[n] = totals[n, :rows, :].astype(f32)
        where = grad_point.at[n // QUARTERS, pl.ds(n % QUARTERS * rows, rows)]
        copies.append(pltpu.make_async_copy(wide.at[n], where, sems.at[n]))
        copies[n].start()
    for n in range(count):
        cell, r = n // QUARTERS, n % QUARTERS
        some = totals[n, rows:rows + 8, :].astype(f32)
        for i in range(3):
            t = 3 * r + i
            if t < 9:
                grad_depth[t, cell:cell + 1, :] = some[i:i + 1]
            elif t == 9:
                grad_gain[cell:cell + 1, :] = some[i:i + 1]
    for copy in copies:
        copy.wait()


def widened(totals, cells, channels):
    count, rows = totals.shape[0], totals.shape[1] - 8
    return pl.pallas_call(
        widen_kernel,
        in_specs=[pl.BlockSpec(memory_space=pltpu.VMEM)],
        out_specs=[pl.BlockSpec(memory_space=pl.ANY)] + [pl.BlockSpec(memory_space=pltpu.VMEM)] * 2,
        out_shape=[
            jax.ShapeDtypeStruct((cells, channels, channels), f32),
            jax.ShapeDtypeStruct((9, cells, channels), f32),
            jax.ShapeDtypeStruct((cells, channels), f32),
        ],
        scratch_shapes=[pltpu.VMEM((count, rows, channels), f32), pltpu.SemaphoreType.DMA((count,))],
        compiler_params=pltpu.CompilerParams(vmem_limit_bytes=12 << 20),
        name="widen",
    )(totals)


def swapped(block):
    return lax.ppermute(block, "section", [(0, 1), (1, 0)])


def exchanged(block, axes):
    return lax.all_to_all(block, axes, 0, 0, tiled=True)


def added(blocks):
    return jnp.sum(blocks.astype(f32), axis=0)


def local(images, cotangent, counts, gains, depthwise, pointwise):
    cells, channels = gains.shape
    section = lax.axis_index("section").astype(jnp.int32)
    point_far = swapped(pointwise)
    vec_own = jnp.concatenate(
        [
            jnp.transpose(depthwise, (1, 0, 2)),
            gains[None],
            jnp.broadcast_to(counts.astype(f32)[:, None, None], (1, cells, channels)),
        ],
        axis=0,
    )
    vec_far = swapped(vec_own)
    images, cotangent, pointwise = (
        pltpu.with_memory_space_constraint(a, pltpu.HBM) for a in (images, cotangent, pointwise)
    )
    kept, sent = run_cells(section[None], images, cotangent, vec_own, vec_far, pointwise, point_far)
    summed = (kept.astype(f32) + swapped(sent).astype(f32)).astype(bf16)

    near, rows, unused = summed.shape
    rows -= 8
    far = lax.axis_size(FAR)
    part = added(exchanged(summed, NEAR))
    strip = part[rows:rows + 4].reshape(-1, LANES)
    strip = jnp.pad(strip, ((0, rows - strip.shape[0]), (0, 0)))
    wide = jnp.concatenate([part[:rows], strip], axis=1).astype(bf16).reshape(far, rows // far, channels + LANES)
    piece = added(exchanged(wide, FAR)).astype(bf16)

    back = exchanged(jnp.broadcast_to(piece, wide.shape), FAR).reshape(rows, channels + LANES)
    small = back[:32, channels:].reshape(8, channels)
    back = jnp.concatenate([back[:, :channels], small], axis=0)
    out = exchanged(jnp.broadcast_to(back, summed.shape), NEAR)
    grad_point, grad_depth, grad_gain = widened(out, cells, channels)
    return grad_point, jnp.transpose(grad_depth, (1, 0, 2)), grad_gain


def solution(mesh):
    grid = Mesh(mesh.devices.reshape(2, 4, 2, 4, 2, 4), ("section", "zh", "zl", "yh", "yl", "x"))
    data = ("zh", "zl", "yh", "yl", "x")
    placed = (
        P(None, data, None, None, None),
        P(None, data, None, None, None),
        P("section"),
        P("section", None),
        P("section", None, None),
        P("section", None, None),
    )
    return jax.shard_map(
        local,
        mesh=grid,
        in_specs=placed,
        out_specs=(P("section", None, None), P("section", None, None), P("section", None)),
        check_vma=False,
    )
```
